32 devices in a mesh: row: 4 (over y, x), col: 8 (over z, core).
Axes of the slice: x: 2, y: 2, z: 4, core: 2. Of those that a mesh axis runs over, the one named last changes fastest.
Arguments:
- teacher: bfloat16 [16384, 256], replicated, may hold values from -4 to 4
- panel_ids: int32 [2048], P('col'), may hold values from 0 to 16383
- rest_ids: int32 [4, 8, 128], P('row', 'col'), may hold values from 0 to 16383
- inverse: bfloat16 [2048, 2048], replicated, may hold values from -1 to 1, as said below
Outputs:
- trailing: float32 [8, 4, 128, 4, 8, 128], P(None, 'row', None, None, 'col')
- panel_rows: bfloat16 [4, 8, 128, 2048], P('row', 'col')
The draws below stay inside these ranges and needn't reach their ends.
Inputs may be any that keep to these rules, and one draw needn't show every extreme that they name: `inverse`: zero above the diagonal.
All inputs are finite; a program needn't handle non-finite values.
Results may differ from the reference program's by a relative error of at most 0.0049.
Values may be sent and summed in bfloat16 or wider, within the bound.
A program may use at most 128 MiB of HBM per device.

```python
import math
import jax
import jax.numpy as jnp
from jax import lax

E = 256
P_SIZE = 2048
VOCAB = 16384
STRETCH = 128
N_ROW = 4
N_COL = 8


def draw_teacher(key, part):
    first_key, second_key = jax.random.split(key, 2)
    groups = 16
    repeats = E // groups
    coords = jnp.clip(jax.random.normal(first_key, (VOCAB, groups), jnp.float32) * math.sqrt(0.5), -3.0, 3.0)
    noise = jnp.clip(0.2 * jax.random.normal(second_key, (VOCAB, E), jnp.float32), -0.8, 0.8)
    tiled = jnp.broadcast_to(coords[:, None, :], (VOCAB, repeats, groups)).reshape(VOCAB, E)
    return jnp.clip(tiled + noise, -4.0, 4.0).astype(jnp.bfloat16)


def draw_inverse(key, part):
    first_key, second_key = jax.random.split(key, 2)
    diagonal = jnp.exp(jax.random.uniform(first_key, (P_SIZE,), jnp.float32, math.log(0.5), math.log(2.0)))
    offdiag = jnp.clip(jax.random.normal(second_key, (P_SIZE, P_SIZE), jnp.float32), -4.0, 4.0)
    places = jnp.arange(P_SIZE)
    lower = places[:, None] > places[None, :]
    matrix = jnp.where(lower, offdiag / math.sqrt(P_SIZE), 0.0) + jnp.diag(diagonal)
    return (matrix * (5.0 / math.sqrt(P_SIZE))).astype(jnp.bfloat16)


def plant(values, rng, low, largest):
    place = [jax.random.randint(jax.random.fold_in(rng, axis), (), 0, length) for axis, length in enumerate(values.shape)]
    main_axis = values.shape.index(max(values.shape))
    neighbour = place[:main_axis] + [(place[main_axis] + 1) % values.shape[main_axis]] + place[main_axis + 1:]
    return values.at[tuple(place)].set(low).at[tuple(neighbour)].set(largest)


def setup_inputs(seed: int = 0) -> dict:
    splits = jax.random.split(jax.random.key(seed), 5)
    teacher = draw_teacher(jax.random.fold_in(splits[4], 71), 0)
    panel_ids = plant(jax.random.randint(splits[1], (P_SIZE,), 0, VOCAB), jax.random.fold_in(splits[1], 1), 0, VOCAB - 1).astype(jnp.int32)
    rest_ids = plant(jax.random.randint(splits[2], (N_ROW, N_COL, STRETCH), 0, VOCAB), jax.random.fold_in(splits[2], 1), 0, VOCAB - 1).astype(jnp.int32)
    inverse = draw_inverse(jax.random.fold_in(splits[4], 71), 0)
    return {"teacher": teacher, "panel_ids": panel_ids, "rest_ids": rest_ids, "inverse": inverse}


def gaussian(left_rows, right_rows, inv_scale):
    sq_left = jnp.sum(jnp.square(left_rows.astype(jnp.float32)), axis=-1)
    sq_right = jnp.sum(jnp.square(right_rows.astype(jnp.float32)), axis=-1)
    inner = lax.dot_general(left_rows, right_rows, (((1,), (1,)), ((), ())), preferred_element_type=jnp.float32)
    return jnp.exp(-inv_scale * (sq_left[:, None] + sq_right[None, :] - 2.0 * inner))


def reference(teacher, panel_ids, rest_ids, inverse):
    inv_scale = 2.0 / E
    panel_emb = teacher[panel_ids]
    rest_emb = teacher[rest_ids.reshape(-1)]
    kernel = gaussian(rest_emb, panel_emb, inv_scale).astype(jnp.bfloat16)
    factors = lax.dot_general(kernel, inverse, (((1,), (1,)), ((), ())), preferred_element_type=jnp.float32).astype(jnp.bfloat16)
    total = rest_emb.shape[0]
    span = total // N_COL

    def one_block(block_at):
        first_row = block_at * span
        left_emb = lax.dynamic_slice_in_dim(rest_emb, first_row, span, 0)
        left_factor = lax.dynamic_slice_in_dim(factors, first_row, span, 0)
        update = lax.dot_general(left_factor, factors, (((1,), (1,)), ((), ())), preferred_element_type=jnp.float32)
        result = gaussian(left_emb, rest_emb, inv_scale) - update
        row_index = first_row + jnp.arange(span, dtype=jnp.int32)
        col_index = jnp.arange(total, dtype=jnp.int32)
        return jnp.where(row_index[:, None] >= col_index[None, :], result, jnp.zeros_like(result))

    full = lax.map(one_block, jnp.arange(N_COL, dtype=jnp.int32))
    trailing = full.reshape(N_COL, N_ROW, STRETCH, N_ROW, N_COL, STRETCH)
    return trailing, factors.reshape(N_ROW, N_COL, STRETCH, P_SIZE)
```

```python
import functools

import jax
import jax.numpy as jnp
from jax import lax
from jax.experimental import pallas as pl
from jax.experimental.pallas import tpu as pltpu
from jax.sharding import PartitionSpec as P

MESH = pl.DeviceIdType.MESH
LANES = 128
VMEM_BYTES = 67043328


def narrow(picked, out, first, count, at):
    halves = out.shape[1] // LANES
    for step in range(0, count, 64):
        for half in range(halves):
            value = picked[pl.ds((first + step) * halves + half, 64, stride=halves), :]
            out[at + step : at + step + 64, half * LANES : (half + 1) * LANES] = value.astype(jnp.bfloat16)


def exchange_kernel(
    n_row, n_col, rest_hbm, panel_hbm, table_hbm, emb_ref, table_ref, rows_out,
    panel_land, col_land, row_land, panel_scaled, col_scaled, panel_ids, col_ids, landed, picked,
    panel_send, row_send, col_send, panel_sem, row_sem, col_sem, table_sem, own_sem, ids_sem,
):
    pieces = table_sem.shape[0]
    halves = table_hbm.shape[1] // LANES
    piece = table_hbm.shape[0] // pieces
    width = panel_land.shape[2]
    stretch = col_land.shape[2]
    row_at = lax.axis_index("row")
    col_at = lax.axis_index("col")
    group = col_at // n_row
    forwards = lax.rem(col_at, n_row) == row_at

    own_panel = pltpu.make_async_copy(panel_hbm.at[0], panel_land.at[col_at], own_sem.at[0])
    own_col = pltpu.make_async_copy(rest_hbm.at[0], col_land.at[row_at], own_sem.at[1])
    own_panel.start()
    own_col.start()

    def load(at):
        rows = pl.ds(at * piece, piece)
        return pltpu.make_async_copy(table_hbm.at[rows], landed.at[rows], table_sem.at[at])

    for at in range(pieces):
        load(at).start()
    barrier = pltpu.get_barrier_semaphore()
    for step in range(1, n_row):
        other = lax.rem(row_at + step, n_row)
        pl.semaphore_signal(barrier, inc=1, device_id=(other, col_at), device_id_type=MESH)
    for step in range(1, n_col):
        other = lax.rem(col_at + step, n_col)
        pl.semaphore_signal(barrier, inc=1, device_id=(row_at, other), device_id_type=MESH)

    def widen(at):
        def body(step, carry):
            rows = pl.ds(pl.multiple_of(at * piece + step * 64, 64), 64)
            wide = landed[rows, :].astype(jnp.float32)
            for half in range(halves):
                place = pl.ds((at * piece + step * 64) * halves + half, 64, stride=halves)
                table_ref[place, :] = wide[:, half * LANES : (half + 1) * LANES]
            return carry

        load(at).wait()
        lax.fori_loop(0, piece // 64, body, 0)

    def panel_copy(slot, target):
        return pltpu.make_async_remote_copy(
            src_ref=panel_land.at[slot], dst_ref=panel_land.at[slot],
            send_sem=panel_send.at[target], recv_sem=panel_sem.at[slot],
            device_id=(row_at, target), device_id_type=MESH,
        )

    def row_copy(slot, target):
        return pltpu.make_async_remote_copy(
            src_ref=col_land, dst_ref=row_land.at[slot],
            send_sem=row_send.at[target], recv_sem=row_sem.at[slot],
            device_id=(row_at, target), device_id_type=MESH,
        )

    def col_copy(slot, target):
        return pltpu.make_async_remote_copy(
            src_ref=col_land.at[slot], dst_ref=col_land.at[slot],
            send_sem=col_send.at[target], recv_sem=col_sem.at[slot],
            device_id=(target, col_at), device_id_type=MESH,
        )

    def each(length, skip, act):
        for at in range(length):
            pl.when(jnp.logical_not(skip(at)))(functools.partial(act, at))

    own_panel.wait()
    own_col.wait()
    pl.semaphore_wait(barrier, n_row + n_col - 2)
    each(n_row, lambda at: at == row_at, lambda at: col_copy(row_at, at).start())
    each(n_col, lambda at: at == col_at, lambda at: panel_copy(col_at, at).start())
    for at in range(pieces):
        widen(at)
    each(n_row, lambda at: at == row_at, lambda at: col_copy(at, at).wait_recv())
    keep = pltpu.make_async_copy(col_land, row_land.at[group], own_sem.at[0])

    @pl.when(forwards)
    def _():
        each(n_col, lambda at: at == col_at, lambda at: row_copy(group, at).start())
        keep.start()

    col_scaled[...] = col_land[...] * halves
    col_move = pltpu.make_async_copy(col_scaled, col_ids, ids_sem.at[0])
    col_move.start()
    each(n_col, lambda at: at == col_at, lambda at: panel_copy(at, at).wait_recv())
    panel_scaled[...] = panel_land[...] * halves
    panel_move = pltpu.make_async_copy(panel_scaled, panel_ids, ids_sem.at[1])
    panel_move.start()

    def pick(ids, block, span, start):
        for lane in range(span):
            place = (start + lane) * halves
            picked[place : place + halves, :] = table_ref[pl.ds(ids[block, 0, lane], halves), :]

    col_move.wait()
    first_col = n_col * width
    for block in range(n_row):
        pick(col_ids, block, stretch, first_col + block * stretch)
    narrow(picked, emb_ref, first_col, n_row * stretch, first_col)
    panel_move.wait()
    for block in range(n_col):
        pick(panel_ids, block, width, block * width)
        if block:
            narrow(picked, emb_ref, (block - 1) * width, width, (block - 1) * width)
    narrow(picked, emb_ref, (n_col - 1) * width, width, (n_col - 1) * width)

    @pl.when(forwards)
    def _():
        keep.wait()

    for slot in range(n_col // n_row):
        source = slot * n_row + row_at

        @pl.when(source != col_at)
        def _(slot=slot, source=source):
            row_copy(slot, source).wait_recv()

    rows_out[...] = row_land[...] * halves
    each(n_row, lambda at: at == row_at, lambda at: col_copy(row_at, at).wait_send())
    each(n_col, lambda at: at == col_at, lambda at: panel_copy(col_at, at).wait_send())

    @pl.when(forwards)
    def _():
        each(n_col, lambda at: at == col_at, lambda at: row_copy(group, at).wait_send())


def exchange(rest_ids, panel_ids, teacher, n_row, n_col):
    stretch = rest_ids.shape[2]
    width = panel_ids.shape[0]
    total = n_col * width + n_row * stretch
    halves = teacher.shape[1] // LANES
    groups = n_col // n_row
    panel_shape = (n_col, 1, width)
    col_shape = (n_row, 1, stretch)
    row_shape = (groups, n_row, 1, stretch)
    vmem = pl.BlockSpec(memory_space=pltpu.VMEM)
    hbm = pl.BlockSpec(memory_space=pltpu.HBM)
    dma = pltpu.SemaphoreType.DMA
    limit = VMEM_BYTES - 4 * teacher.size - 2 * total * teacher.shape[1] - 12 * 1024 * 1024
    return pl.pallas_call(
        functools.partial(exchange_kernel, n_row, n_col),
        out_shape=(
            jax.ShapeDtypeStruct((total, teacher.shape[1]), teacher.dtype),
            jax.ShapeDtypeStruct((teacher.shape[0] * halves, LANES), jnp.float32),
            jax.ShapeDtypeStruct(row_shape, jnp.int32),
        ),
        in_specs=[hbm, hbm, hbm],
        out_specs=(vmem, vmem, vmem),
        scratch_shapes=[
            pltpu.VMEM(panel_shape, jnp.int32),
            pltpu.VMEM(col_shape, jnp.int32),
            pltpu.VMEM(row_shape, jnp.int32),
            pltpu.VMEM(panel_shape, jnp.int32),
            pltpu.VMEM(col_shape, jnp.int32),
            pltpu.SMEM(panel_shape, jnp.int32),
            pltpu.SMEM(col_shape, jnp.int32),
            pltpu.VMEM(teacher.shape, teacher.dtype),
            pltpu.VMEM((total * halves, LANES), jnp.float32),
            dma((n_col,)), dma((n_col,)), dma((n_row,)),
            dma((n_col,)), dma((groups,)), dma((n_row,)),
            dma((8,)), dma((2,)), dma((2,)),
        ],
        compiler_params=pltpu.CompilerParams(
            collective_id=0, has_side_effects=True, vmem_limit_bytes=limit
        ),
        name="exchange",
    )(*(pltpu.with_memory_space_constraint(x, pltpu.HBM) for x in (rest_ids, panel_ids.reshape(1, 1, width), teacher)))


def nt_dot(left, right):
    return lax.dot_general(left, right, (((1,), (1,)), ((), ())), preferred_element_type=jnp.float32)


def nn_dot(left, right):
    return lax.dot_general(left, right, (((1,), (0,)), ((), ())), preferred_element_type=jnp.float32)


def gram_kernel(
    n_row, n_col, stretch, emb_ref, rows_in, table_ref, inv_hbm, trail_hbm, own_hbm,
    row_ids, picked, left_ref, inv_ref, cross_ref, fac_ref, back_ref, norm_ref, trail_ref,
    inv_sem, ids_sem, own_sem, trail_sem,
):
    width = inv_hbm.shape[0]
    block = 256
    blocks = width // block
    embed = emb_ref.shape[1]
    halves = embed // LANES
    n_rows = n_col * stretch
    n_cols = n_row * stretch
    groups = n_col // n_row
    unit = 2.0 / embed * 1.4426950408889634
    row_at = lax.axis_index("row")
    col_at = lax.axis_index("col")
    tile = 512

    ids_move = pltpu.make_async_copy(rows_in, row_ids, ids_sem)
    ids_move.start()

    def load(at):
        rows, cols = pl.ds(at * block, block), pl.ds(0, (at + 1) * block)
        return pltpu.make_async_copy(inv_hbm.at[rows, cols], inv_ref.at[rows, cols], inv_sem.at[at])

    for at in range(blocks):
        load(at).start()

    eye = lax.broadcasted_iota(jnp.int32, (LANES, LANES), 0) == lax.broadcasted_iota(jnp.int32, (LANES, LANES), 1)

    def down(value):
        return jnp.sum(jnp.square(value.astype(jnp.float32)), axis=-1, keepdims=True) * unit

    def across(start, count):
        for at in range(start, start + count, LANES):
            norm = jnp.broadcast_to(down(emb_ref[at : at + LANES, :]), (LANES, LANES))
            norm_ref[0:1, at : at + LANES] = jnp.sum(jnp.where(eye, norm, 0.0), axis=0, keepdims=True)

    def gram(left, left_norm, start, count):
        right, right_norm = emb_ref[start : start + count, :], norm_ref[0:1, start : start + count]
        return jnp.exp2(nt_dot(left, right) * (2.0 * unit) - (left_norm + right_norm))

    def pick(start, count):
        for row in range(start, start + count):
            q, lane = divmod(row, stretch)
            place = table_ref[pl.ds(row_ids[q % groups, q // groups, 0, lane], halves), :]
            picked[row * halves : (row + 1) * halves, :] = place
        narrow(picked, left_ref, start, count, start)

    share = n_rows * tile // (n_cols * blocks)
    ids_move.wait()
    done = 0
    for start in range(0, n_cols, tile):
        left = emb_ref[width + start : width + start + tile, :]
        left_norm = down(left)
        rows = slice(start, start + tile)
        for at in range(blocks):
            cols = slice(at * block, (at + 1) * block)
            if not start:
                across(at * block, block)
            cross_ref[:, cols] = gram(left, left_norm, at * block, block).astype(jnp.bfloat16)
            if not start:
                load(at).wait()
            fac_ref[rows, cols] = nt_dot(
                cross_ref[:, : (at + 1) * block], inv_ref[cols, : (at + 1) * block]
            ).astype(jnp.bfloat16)
            pick(done, share)
            done += share
    own = pltpu.make_async_copy(
        fac_ref.at[pl.ds(pl.multiple_of(row_at * stretch, stretch), stretch), :], own_hbm, own_sem
    )
    own.start()
    across(width, n_cols)
    for start in range(0, n_cols, tile):
        rows = slice(start, start + tile)
        for at in range(blocks):
            cols = slice(at * block, (at + 1) * block)
            back_ref[rows, cols] = nn_dot(fac_ref[rows, at * block :], inv_ref[at * block :, cols]).astype(jnp.bfloat16)

    ahead = lax.broadcasted_iota(jnp.int32, (stretch, stretch), 0) - lax.broadcasted_iota(
        jnp.int32, (stretch, stretch), 1
    )
    pair = 2 if n_row % 2 == 0 else 1

    def flush(start):
        first, count = start // stretch, tile // stretch
        span = pl.ds(first * stretch * n_row, count * stretch * n_row)
        return pltpu.make_async_copy(trail_ref.at[span], trail_hbm.at[span], trail_sem.at[start // tile])

    for start in range(0, n_rows, tile):
        left = left_ref[start : start + tile, :]
        left_norm = down(left)
        last = (start + tile) // stretch - 1
        for at in range(blocks):
            cross_ref[:, at * block : (at + 1) * block] = gram(left, left_norm, at * block, block).astype(jnp.bfloat16)
        for low in range(0, n_row, pair):
            if last * n_row + n_row - 1 >= low * n_col:
                span = slice(low * stretch, (low + pair) * stretch)
                value = gram(left, left_norm, width + low * stretch, pair * stretch) - nt_dot(
                    cross_ref[...], back_ref[span, :]
                )
            else:
                value = None
            for q in range(start // stretch, last + 1):
                for p in range(low, low + pair):
                    place = pl.ds(q * stretch * n_row + p, stretch, stride=n_row)
                    if q * n_row + n_row - 1 < p * n_col:
                        trail_ref[place, :] = jnp.zeros((stretch, stretch), jnp.float32)
                    else:
                        top = q * stretch - start
                        side = (p - low) * stretch
                        part = value[top : top + stretch, side : side + stretch]
                        gap = (p * n_col + col_at - q * n_row - row_at) * stretch
                        trail_ref[place, :] = jnp.where(ahead >= gap, part, 0.0)
        flush(start).start()
    own.wait()
    for start in range(0, n_rows, tile):
        flush(start).wait()


def shards(teacher, panel_ids, rest_ids, inverse):
    n_row = lax.axis_size("row")
    n_col = lax.axis_size("col")
    stretch = rest_ids.shape[2]
    width = inverse.shape[0]
    emb, table, rows = exchange(rest_ids, panel_ids, teacher, n_row, n_col)
    n_rows = n_col * stretch
    n_cols = n_row * stretch
    embed = teacher.shape[1]
    halves = embed // LANES
    vmem = pl.BlockSpec(memory_space=pltpu.VMEM)
    hbm = pl.BlockSpec(memory_space=pltpu.HBM)
    dma = pltpu.SemaphoreType.DMA
    limit = VMEM_BYTES - 4 * teacher.size - 2 * (width + n_cols) * embed - 12 * 1024 * 1024
    trailing, own_factor = pl.pallas_call(
        functools.partial(gram_kernel, n_row, n_col, stretch),
        out_shape=(
            jax.ShapeDtypeStruct((n_rows * n_row, stretch), jnp.float32),
            jax.ShapeDtypeStruct((stretch, width), jnp.bfloat16),
        ),
        in_specs=[vmem, vmem, vmem, hbm],
        out_specs=(hbm, hbm),
        scratch_shapes=[
            pltpu.SMEM(rows.shape, jnp.int32),
            pltpu.VMEM((n_rows * halves, LANES), jnp.float32),
            pltpu.VMEM((n_rows, embed), jnp.bfloat16),
            pltpu.VMEM((width, width), jnp.bfloat16),
            pltpu.VMEM((512, width), jnp.bfloat16),
            pltpu.VMEM((n_cols, width), jnp.bfloat16),
            pltpu.VMEM((n_cols, width), jnp.bfloat16),
            pltpu.VMEM((8, width + n_cols), jnp.float32),
            pltpu.VMEM((n_rows * n_row, stretch), jnp.float32),
            dma((width // 256,)), dma(()), dma(()), dma((n_rows // 512,)),
        ],
        compiler_params=pltpu.CompilerParams(vmem_limit_bytes=limit),
        name="gram",
    )(emb, rows, table, pltpu.with_memory_space_constraint(inverse, pltpu.HBM))
    return (
        trailing.reshape(n_col, 1, stretch, n_row, 1, stretch),
        own_factor.reshape(1, 1, stretch, width),
    )


def solution(mesh):
    return jax.shard_map(
        shards,
        mesh=mesh,
        in_specs=(P(), P("col"), P("row", "col", None), P()),
        out_specs=(P(None, "row", None, None, "col", None), P("row", "col", None, None)),
        check_vma=False,
    )
```

```python
import functools

import jax
import jax.numpy as jnp
from jax import lax
from jax.experimental import pallas as pl
from jax.experimental.pallas import tpu as pltpu
from jax.sharding import PartitionSpec as P

MESH = pl.DeviceIdType.MESH
LANES = 128
VMEM_BYTES = 67043328


def narrow(picked, out, first, count, at):
    halves = out.shape[1] // LANES
    for step in range(0, count, 64):
        for half in range(halves):
            value = picked[pl.ds((first + step) * halves + half, 64, stride=halves), :]
            out[at + step : at + step + 64, half * LANES : (half + 1) * LANES] = value.astype(jnp.bfloat16)


def exchange_kernel(
    n_row, n_col, rest_hbm, panel_hbm, table_hbm, inv_hbm, emb_ref, table_ref, rows_out, inv_ref,
    panel_land, col_land, row_land, panel_scaled, col_scaled, panel_ids, col_ids, landed, picked,
    panel_send, row_send, col_send, panel_sem, row_sem, col_sem, table_sem, inv_sem, own_sem, ids_sem,
):
    pieces = table_sem.shape[0]
    halves = table_hbm.shape[1] // LANES
    piece = table_hbm.shape[0] // pieces
    width = panel_land.shape[2]
    stretch = col_land.shape[2]
    row_at = lax.axis_index("row")
    col_at = lax.axis_index("col")
    group = col_at // n_row
    forwards = lax.rem(col_at, n_row) == row_at

    own_panel = pltpu.make_async_copy(panel_hbm.at[0], panel_land.at[col_at], own_sem.at[0])
    own_col = pltpu.make_async_copy(rest_hbm.at[0], col_land.at[row_at], own_sem.at[1])
    own_panel.start()
    own_col.start()

    def load(at):
        rows = pl.ds(at * piece, piece)
        return pltpu.make_async_copy(table_hbm.at[rows], landed.at[rows], table_sem.at[at])

    def load_inverse(at):
        block = inv_hbm.shape[0] // pieces
        rows, cols = pl.ds(at * block, block), pl.ds(0, (at + 1) * block)
        return pltpu.make_async_copy(inv_hbm.at[rows, cols], inv_ref.at[rows, cols], inv_sem.at[at])

    for at in range(pieces):
        load(at).start()
    for at in range(pieces):
        load_inverse(at).start()
    barrier = pltpu.get_barrier_semaphore()
    for step in range(1, n_row):
        other = lax.rem(row_at + step, n_row)
        pl.semaphore_signal(barrier, inc=1, device_id=(other, col_at), device_id_type=MESH)
    for step in range(1, n_col):
        other = lax.rem(col_at + step, n_col)
        pl.semaphore_signal(barrier, inc=1, device_id=(row_at, other), device_id_type=MESH)

    def widen(at):
        def body(step, carry):
            rows = pl.ds(pl.multiple_of(at * piece + step * 64, 64), 64)
            wide = landed[rows, :].astype(jnp.float32)
            for half in range(halves):
                place = pl.ds((at * piece + step * 64) * halves + half, 64, stride=halves)
                table_ref[place, :] = wide[:, half * LANES : (half + 1) * LANES]
            return carry

        load(at).wait()
        lax.fori_loop(0, piece // 64, body, 0)

    def panel_copy(slot, target):
        return pltpu.make_async_remote_copy(
            src_ref=panel_land.at[slot], dst_ref=panel_land.at[slot],
            send_sem=panel_send.at[target], recv_sem=panel_sem.at[slot],
            device_id=(row_at, target), device_id_type=MESH,
        )

    def row_copy(slot, target):
        return pltpu.make_async_remote_copy(
            src_ref=col_land, dst_ref=row_land.at[slot],
            send_sem=row_send.at[target], recv_sem=row_sem.at[slot],
            device_id=(row_at, target), device_id_type=MESH,
        )

    def col_copy(slot, target):
        return pltpu.make_async_remote_copy(
            src_ref=col_land.at[slot], dst_ref=col_land.at[slot],
            send_sem=col_send.at[target], recv_sem=col_sem.at[slot],
            device_id=(target, col_at), device_id_type=MESH,
        )

    def each(length, skip, act):
        for at in range(length):
            pl.when(jnp.logical_not(skip(at)))(functools.partial(act, at))

    own_panel.wait()
    own_col.wait()
    pl.semaphore_wait(barrier, n_row + n_col - 2)
    each(n_row, lambda at: at == row_at, lambda at: col_copy(row_at, at).start())
    each(n_col, lambda at: at == col_at, lambda at: panel_copy(col_at, at).start())
    for at in range(pieces):
        widen(at)
    each(n_row, lambda at: at == row_at, lambda at: col_copy(at, at).wait_recv())
    keep = pltpu.make_async_copy(col_land, row_land.at[group], own_sem.at[0])

    @pl.when(forwards)
    def _():
        each(n_col, lambda at: at == col_at, lambda at: row_copy(group, at).start())
        keep.start()

    col_scaled[...] = col_land[...] * halves
    col_move = pltpu.make_async_copy(col_scaled, col_ids, ids_sem.at[0])
    col_move.start()
    each(n_col, lambda at: at == col_at, lambda at: panel_copy(at, at).wait_recv())
    panel_scaled[...] = panel_land[...] * halves
    panel_move = pltpu.make_async_copy(panel_scaled, panel_ids, ids_sem.at[1])
    panel_move.start()

    def pick(ids, block, span, start):
        for lane in range(span):
            place = (start + lane) * halves
            picked[place : place + halves, :] = table_ref[pl.ds(ids[block, 0, lane], halves), :]

    col_move.wait()
    first_col = n_col * width
    for block in range(n_row):
        pick(col_ids, block, stretch, first_col + block * stretch)
    narrow(picked, emb_ref, first_col, n_row * stretch, first_col)
    panel_move.wait()
    for block in range(n_col):
        pick(panel_ids, block, width, block * width)
        if block:
            narrow(picked, emb_ref, (block - 1) * width, width, (block - 1) * width)
    narrow(picked, emb_ref, (n_col - 1) * width, width, (n_col - 1) * width)

    @pl.when(forwards)
    def _():
        keep.wait()

    for slot in range(n_col // n_row):
        source = slot * n_row + row_at

        @pl.when(source != col_at)
        def _(slot=slot, source=source):
            row_copy(slot, source).wait_recv()

    rows_out[...] = row_land[...] * halves
    for at in range(pieces):
        load_inverse(at).wait()
    each(n_row, lambda at: at == row_at, lambda at: col_copy(row_at, at).wait_send())
    each(n_col, lambda at: at == col_at, lambda at: panel_copy(col_at, at).wait_send())

    @pl.when(forwards)
    def _():
        each(n_col, lambda at: at == col_at, lambda at: row_copy(group, at).wait_send())


def own_limit(teacher, inverse, total):
    return VMEM_BYTES - 4 * teacher.size - 2 * inverse.size - 2 * total * teacher.shape[1] - 12 * 1024 * 1024


def exchange(rest_ids, panel_ids, teacher, inverse, n_row, n_col):
    stretch = rest_ids.shape[2]
    width = panel_ids.shape[0]
    total = n_col * width + n_row * stretch
    halves = teacher.shape[1] // LANES
    groups = n_col // n_row
    panel_shape = (n_col, 1, width)
    col_shape = (n_row, 1, stretch)
    row_shape = (groups, n_row, 1, stretch)
    vmem = pl.BlockSpec(memory_space=pltpu.VMEM)
    hbm = pl.BlockSpec(memory_space=pltpu.HBM)
    dma = pltpu.SemaphoreType.DMA
    operands = (rest_ids, panel_ids.reshape(1, 1, width), teacher, inverse)
    return pl.pallas_call(
        functools.partial(exchange_kernel, n_row, n_col),
        out_shape=(
            jax.ShapeDtypeStruct((total, teacher.shape[1]), teacher.dtype),
            jax.ShapeDtypeStruct((teacher.shape[0] * halves, LANES), jnp.float32),
            jax.ShapeDtypeStruct(row_shape, jnp.int32),
            jax.ShapeDtypeStruct(inverse.shape, inverse.dtype),
        ),
        in_specs=[hbm] * 4,
        out_specs=(vmem,) * 4,
        scratch_shapes=[
            pltpu.VMEM(panel_shape, jnp.int32),
            pltpu.VMEM(col_shape, jnp.int32),
            pltpu.VMEM(row_shape, jnp.int32),
            pltpu.VMEM(panel_shape, jnp.int32),
            pltpu.VMEM(col_shape, jnp.int32),
            pltpu.SMEM(panel_shape, jnp.int32),
            pltpu.SMEM(col_shape, jnp.int32),
            pltpu.VMEM(teacher.shape, teacher.dtype),
            pltpu.VMEM((total * halves, LANES), jnp.float32),
            dma((n_col,)), dma((n_col,)), dma((n_row,)),
            dma((n_col,)), dma((groups,)), dma((n_row,)),
            dma((8,)), dma((8,)), dma((2,)), dma((2,)),
        ],
        compiler_params=pltpu.CompilerParams(
            collective_id=0, has_side_effects=True, vmem_limit_bytes=own_limit(teacher, inverse, total)
        ),
        name="exchange",
    )(*(pltpu.with_memory_space_constraint(x, pltpu.HBM) for x in operands))


def nt_dot(left, right):
    return lax.dot_general(left, right, (((1,), (1,)), ((), ())), preferred_element_type=jnp.float32)


def nn_dot(left, right):
    return lax.dot_general(left, right, (((1,), (0,)), ((), ())), preferred_element_type=jnp.float32)


def gram_kernel(
    n_row, n_col, stretch, emb_ref, rows_in, table_ref, inv_ref, trail_hbm, own_hbm,
    row_ids, picked, left_ref, cross_ref, fac_ref, back_ref, norm_ref, trail_ref,
    ids_sem, own_sem, trail_sem,
):
    width = inv_ref.shape[0]
    block = 256
    blocks = width // block
    embed = emb_ref.shape[1]
    halves = embed // LANES
    n_rows = n_col * stretch
    n_cols = n_row * stretch
    groups = n_col // n_row
    unit = 2.0 / embed * 1.4426950408889634
    row_at = lax.axis_index("row")
    col_at = lax.axis_index("col")
    tile = 512
    chunk = 64
    ring = picked.shape[0] // (chunk * halves)

    ids_move = pltpu.make_async_copy(rows_in, row_ids, ids_sem)
    ids_move.start()
    eye = lax.broadcasted_iota(jnp.int32, (LANES, LANES), 0) == lax.broadcasted_iota(jnp.int32, (LANES, LANES), 1)

    def down(value):
        return jnp.sum(jnp.square(value.astype(jnp.float32)), axis=-1, keepdims=True) * unit

    def across(start, count):
        for at in range(start, start + count, LANES):
            norm = jnp.broadcast_to(down(emb_ref[at : at + LANES, :]), (LANES, LANES))
            norm_ref[0:1, at : at + LANES] = jnp.sum(jnp.where(eye, norm, 0.0), axis=0, keepdims=True)

    def inner(left, start, count):
        return nt_dot(left, emb_ref[start : start + count, :])

    def gaussian(product, left_norm, start, count):
        return jnp.exp2(product * (2.0 * unit) - (left_norm + norm_ref[0:1, start : start + count]))

    def pick(start, count):
        for base in range(start, start + count, chunk):
            home = base // chunk % ring * chunk
            for lane in range(chunk):
                q, place = divmod(base + lane, stretch)
                row = table_ref[pl.ds(row_ids[q % groups, q // groups, 0, place], halves), :]
                picked[(home + lane) * halves : (home + lane + 1) * halves, :] = row
            narrow(picked, left_ref, home, chunk, base)

    picked_rows = 0
    hold = slice(tile, 2 * tile)
    for start in range(0, n_cols, tile):
        left = emb_ref[width + start : width + start + tile, :]
        left_norm = down(left)
        rows = slice(start, start + tile)
        product = inner(left, 0, block)
        for at in range(blocks + 1):
            cols = slice((at - 1) * block, at * block)
            held = product
            if at < blocks:
                here = slice(at * block, (at + 1) * block)
                if not start:
                    across(at * block, block)
                cross_ref[hold, here] = gaussian(held, left_norm, at * block, block).astype(jnp.bfloat16)
                if at + 1 < blocks:
                    product = inner(left, (at + 1) * block, block)
            if at:
                if at == 1 and not start:
                    ids_move.wait()
                fac_ref[rows, cols] = nt_dot(
                    cross_ref[hold, : at * block], inv_ref[cols, : at * block]
                ).astype(jnp.bfloat16)
                if not start:
                    until = n_rows * at * (at + 1) // (blocks * (blocks + 1)) // chunk * chunk
                    pick(picked_rows, until - picked_rows)
                    picked_rows = until
    own = pltpu.make_async_copy(
        fac_ref.at[pl.ds(pl.multiple_of(row_at * stretch, stretch), stretch), :], own_hbm, own_sem
    )
    own.start()
    across(width, n_cols)
    lefts = [(start, down(left_ref[start : start + tile, :])) for start in range(0, n_rows, tile)]

    def cross_rows(tile_at, at):
        start, left_norm = lefts[tile_at]
        product = inner(left_ref[start : start + tile, :], at * block, block)
        value = gaussian(product, left_norm, at * block, block)
        home = tile_at % 2 * tile
        cross_ref[home : home + tile, at * block : (at + 1) * block] = value.astype(jnp.bfloat16)

    for at in range(blocks):
        cols = slice(at * block, (at + 1) * block)
        for tile_at in range(min(2, len(lefts))):
            cross_rows(tile_at, at)
        for start in range(0, n_cols, tile):
            rows = slice(start, start + tile)
            back_ref[rows, cols] = nn_dot(fac_ref[rows, at * block :], inv_ref[at * block :, cols]).astype(jnp.bfloat16)

    ahead = lax.broadcasted_iota(jnp.int32, (stretch, stretch), 0) - lax.broadcasted_iota(
        jnp.int32, (stretch, stretch), 1
    )
    pair = 2 if n_row % 2 == 0 else 1
    held_rows = tile * n_row

    def flush(at):
        return pltpu.make_async_copy(
            trail_ref.at[pl.ds(at % 2 * held_rows, held_rows)], trail_hbm.at[pl.ds(at * held_rows, held_rows)],
            trail_sem.at[at % 2],
        )

    for tile_at, (start, left_norm) in enumerate(lefts):
        left = left_ref[start : start + tile, :]
        last = (start + tile) // stretch - 1
        if tile_at >= 2:
            flush(tile_at - 2).wait()
            for at in range(blocks):
                cross_rows(tile_at, at)
        home = tile_at % 2 * tile
        for low in range(0, n_row, pair):
            if last * n_row + n_row - 1 >= low * n_col:
                span = slice(low * stretch, (low + pair) * stretch)
                first = width + low * stretch
                value = gaussian(inner(left, first, pair * stretch), left_norm, first, pair * stretch) - nt_dot(
                    cross_ref[home : home + tile, :], back_ref[span, :]
                )
            else:
                value = None
            for q in range(start // stretch, last + 1):
                for p in range(low, low + pair):
                    top = q * stretch - start
                    place = pl.ds(tile_at % 2 * held_rows + top * n_row + p, stretch, stride=n_row)
                    if q * n_row + n_row - 1 < p * n_col:
                        trail_ref[place, :] = jnp.zeros((stretch, stretch), jnp.float32)
                        continue
                    side = (p - low) * stretch
                    part = value[top : top + stretch, side : side + stretch]
                    if q * n_row < p * n_col + n_col:
                        gap = (p * n_col + col_at - q * n_row - row_at) * stretch
                        part = jnp.where(ahead >= gap, part, 0.0)
                    trail_ref[place, :] = part
        flush(tile_at).start()
    own.wait()
    for tile_at in range(max(len(lefts) - 2, 0), len(lefts)):
        flush(tile_at).wait()


def shards(teacher, panel_ids, rest_ids, inverse):
    n_row = lax.axis_size("row")
    n_col = lax.axis_size("col")
    stretch = rest_ids.shape[2]
    width = inverse.shape[0]
    emb, table, rows, inv = exchange(rest_ids, panel_ids, teacher, inverse, n_row, n_col)
    n_rows = n_col * stretch
    n_cols = n_row * stretch
    embed = teacher.shape[1]
    halves = embed // LANES
    vmem = pl.BlockSpec(memory_space=pltpu.VMEM)
    hbm = pl.BlockSpec(memory_space=pltpu.HBM)
    dma = pltpu.SemaphoreType.DMA
    limit = own_limit(teacher, inverse, width + n_cols)
    held = 2 * n_rows * embed + 2048 * width + 4 * n_cols * width + 4096 * n_row * stretch + 9 * 1024 * 1024
    trailing, own_factor = pl.pallas_call(
        functools.partial(gram_kernel, n_row, n_col, stretch),
        out_shape=(
            jax.ShapeDtypeStruct((n_rows * n_row, stretch), jnp.float32),
            jax.ShapeDtypeStruct((stretch, width), jnp.bfloat16),
        ),
        in_specs=[vmem] * 4,
        out_specs=(hbm, hbm),
        scratch_shapes=[
            pltpu.SMEM(rows.shape, jnp.int32),
            pltpu.VMEM((512 * halves, LANES), jnp.float32),
            pltpu.VMEM((n_rows, embed), jnp.bfloat16),
            pltpu.VMEM((2 * 512, width), jnp.bfloat16),
            pltpu.VMEM((n_cols, width), jnp.bfloat16),
            pltpu.VMEM((n_cols, width), jnp.bfloat16),
            pltpu.VMEM((8, width + n_cols), jnp.float32),
            pltpu.VMEM((2 * 512 * n_row, stretch), jnp.float32),
            dma(()), dma(()), dma((2,)),
        ],
        compiler_params=pltpu.CompilerParams(vmem_limit_bytes=max(limit, held)),
        name="gram",
    )(emb, rows, table, inv)
    return (
        trailing.reshape(n_col, 1, stretch, n_row, 1, stretch),
        own_factor.reshape(1, 1, stretch, width),
    )


def solution(mesh):
    return jax.shard_map(
        shards,
        mesh=mesh,
        in_specs=(P(), P("col"), P("row", "col", None), P()),
        out_specs=(P(None, "row", None, None, "col", None), P("row", "col", None, None)),
        check_vma=False,
    )
```

```python
import functools

import jax
import jax.numpy as jnp
from jax import lax
from jax.experimental import pallas as pl
from jax.experimental.pallas import tpu as pltpu
from jax.sharding import PartitionSpec as P

MESH = pl.DeviceIdType.MESH
LANES = 128
VMEM_BYTES = 67043328


def narrow(picked, out, first, count, at):
    halves = out.shape[1] // LANES
    for step in range(0, count, 64):
        for half in range(halves):
            value = picked[pl.ds((first + step) * halves + half, 64, stride=halves), :]
            out[at + step : at + step + 64, half * LANES : (half + 1) * LANES] = value.astype(jnp.bfloat16)


def unit_of(embed):
    return 2.0 / embed * 1.4426950408889634


def row_norm(value):
    return jnp.sum(jnp.square(value.astype(jnp.float32)), axis=-1, keepdims=True) * unit_of(value.shape[1])


def exchange_kernel(
    n_row, n_col, rest_hbm, panel_hbm, table_hbm, inv_hbm, emb_ref, table_ref, rows_out, inv_ref, norm_ref,
    panel_land, col_land, row_land, panel_scaled, col_scaled, panel_ids, col_ids, landed, picked,
    panel_send, row_send, col_send, panel_sem, row_sem, col_sem, table_sem, inv_sem, own_sem, ids_sem,
):
    pieces = table_sem.shape[0]
    halves = table_hbm.shape[1] // LANES
    piece = table_hbm.shape[0] // pieces
    width = panel_land.shape[2]
    stretch = col_land.shape[2]
    row_at = lax.axis_index("row")
    col_at = lax.axis_index("col")
    group = col_at // n_row
    forwards = lax.rem(col_at, n_row) == row_at

    own_panel = pltpu.make_async_copy(panel_hbm.at[0], panel_land.at[col_at], own_sem.at[0])
    own_col = pltpu.make_async_copy(rest_hbm.at[0], col_land.at[row_at], own_sem.at[1])
    own_panel.start()
    own_col.start()

    def load(at):
        rows = pl.ds(at * piece, piece)
        return pltpu.make_async_copy(table_hbm.at[rows], landed.at[rows], table_sem.at[at])

    def load_inverse(at):
        block = inv_hbm.shape[0] // pieces
        rows, cols = pl.ds(at * block, block), pl.ds(0, (at + 1) * block)
        return pltpu.make_async_copy(inv_hbm.at[rows, cols], inv_ref.at[rows, cols], inv_sem.at[at])

    for at in range(pieces):
        load(at).start()
    barrier = pltpu.get_barrier_semaphore()
    for step in range(1, n_row):
        other = lax.rem(row_at + step, n_row)
        pl.semaphore_signal(barrier, inc=1, device_id=(other, col_at), device_id_type=MESH)
    for step in range(1, n_col):
        other = lax.rem(col_at + step, n_col)
        pl.semaphore_signal(barrier, inc=1, device_id=(row_at, other), device_id_type=MESH)

    def widen(at):
        def body(step, carry):
            rows = pl.ds(pl.multiple_of(at * piece + step * 64, 64), 64)
            wide = landed[rows, :].astype(jnp.float32)
            for half in range(halves):
                place = pl.ds((at * piece + step * 64) * halves + half, 64, stride=halves)
                table_ref[place, :] = wide[:, half * LANES : (half + 1) * LANES]
            return carry

        load(at).wait()
        lax.fori_loop(0, piece // 64, body, 0)

    def panel_copy(slot, target):
        return pltpu.make_async_remote_copy(
            src_ref=panel_land.at[slot], dst_ref=panel_land.at[slot],
            send_sem=panel_send.at[target], recv_sem=panel_sem.at[slot],
            device_id=(row_at, target), device_id_type=MESH,
        )

    def row_copy(slot, target):
        return pltpu.make_async_remote_copy(
            src_ref=col_land, dst_ref=row_land.at[slot],
            send_sem=row_send.at[target], recv_sem=row_sem.at[slot],
            device_id=(row_at, target), device_id_type=MESH,
        )

    def col_copy(slot, target):
        return pltpu.make_async_remote_copy(
            src_ref=col_land.at[slot], dst_ref=col_land.at[slot],
            send_sem=col_send.at[target], recv_sem=col_sem.at[slot],
            device_id=(target, col_at), device_id_type=MESH,
        )

    def each(length, skip, act):
        for at in range(length):
            pl.when(jnp.logical_not(skip(at)))(functools.partial(act, at))

    own_panel.wait()
    own_col.wait()
    pl.semaphore_wait(barrier, n_row + n_col - 2)
    each(n_row, lambda at: at == row_at, lambda at: col_copy(row_at, at).start())
    each(n_col, lambda at: at == col_at, lambda at: panel_copy(col_at, at).start())
    for at in range(pieces // 2):
        widen(at)
    each(n_row, lambda at: at == row_at, lambda at: col_copy(at, at).wait_recv())
    keep = pltpu.make_async_copy(col_land, row_land.at[group], own_sem.at[0])

    @pl.when(forwards)
    def _():
        each(n_col, lambda at: at == col_at, lambda at: row_copy(group, at).start())
        keep.start()

    col_scaled[...] = col_land[...] * halves
    col_move = pltpu.make_async_copy(col_scaled, col_ids, ids_sem.at[0])
    col_move.start()
    for at in range(pieces):
        load_inverse(at).start()
    for at in range(pieces // 2, pieces):
        widen(at)
    each(n_col, lambda at: at == col_at, lambda at: panel_copy(at, at).wait_recv())
    panel_scaled[...] = panel_land[...] * halves
    panel_move = pltpu.make_async_copy(panel_scaled, panel_ids, ids_sem.at[1])
    panel_move.start()

    def pick(ids, block, span, start):
        for lane in range(span):
            place = (start + lane) * halves
            picked[place : place + halves, :] = table_ref[pl.ds(ids[block, 0, lane], halves), :]

    col_move.wait()
    first_col = n_col * width
    for block in range(n_row):
        pick(col_ids, block, stretch, first_col + block * stretch)
    narrow(picked, emb_ref, first_col, n_row * stretch, first_col)
    panel_move.wait()
    for block in range(n_col):
        pick(panel_ids, block, width, block * width)
        if block:
            narrow(picked, emb_ref, (block - 1) * width, width, (block - 1) * width)
    narrow(picked, emb_ref, (n_col - 1) * width, width, (n_col - 1) * width)
    eye = lax.broadcasted_iota(jnp.int32, (LANES, LANES), 0) == lax.broadcasted_iota(jnp.int32, (LANES, LANES), 1)
    for at in range(0, emb_ref.shape[0], LANES):
        norm = jnp.broadcast_to(row_norm(emb_ref[at : at + LANES, :]), (LANES, LANES))
        norm_ref[0:1, at : at + LANES] = jnp.sum(jnp.where(eye, norm, 0.0), axis=0, keepdims=True)

    @pl.when(forwards)
    def _():
        keep.wait()

    for slot in range(n_col // n_row):
        source = slot * n_row + row_at

        @pl.when(source != col_at)
        def _(slot=slot, source=source):
            row_copy(slot, source).wait_recv()

    rows_out[...] = row_land[...] * halves
    for at in range(pieces):
        load_inverse(at).wait()
    each(n_row, lambda at: at == row_at, lambda at: col_copy(row_at, at).wait_send())
    each(n_col, lambda at: at == col_at, lambda at: panel_copy(col_at, at).wait_send())

    @pl.when(forwards)
    def _():
        each(n_col, lambda at: at == col_at, lambda at: row_copy(group, at).wait_send())


def own_limit(teacher, inverse, total):
    return VMEM_BYTES - 4 * teacher.size - 2 * inverse.size - 2 * total * teacher.shape[1] - 12 * 1024 * 1024


def exchange(rest_ids, panel_ids, teacher, inverse, n_row, n_col):
    stretch = rest_ids.shape[2]
    width = panel_ids.shape[0]
    total = n_col * width + n_row * stretch
    halves = teacher.shape[1] // LANES
    groups = n_col // n_row
    panel_shape = (n_col, 1, width)
    col_shape = (n_row, 1, stretch)
    row_shape = (groups, n_row, 1, stretch)
    vmem = pl.BlockSpec(memory_space=pltpu.VMEM)
    hbm = pl.BlockSpec(memory_space=pltpu.HBM)
    dma = pltpu.SemaphoreType.DMA
    operands = (rest_ids, panel_ids.reshape(1, 1, width), teacher, inverse)
    return pl.pallas_call(
        functools.partial(exchange_kernel, n_row, n_col),
        out_shape=(
            jax.ShapeDtypeStruct((total, teacher.shape[1]), teacher.dtype),
            jax.ShapeDtypeStruct((teacher.shape[0] * halves, LANES), jnp.float32),
            jax.ShapeDtypeStruct(row_shape, jnp.int32),
            jax.ShapeDtypeStruct(inverse.shape, inverse.dtype),
            jax.ShapeDtypeStruct((8, total), jnp.float32),
        ),
        in_specs=[hbm] * 4,
        out_specs=(vmem,) * 5,
        scratch_shapes=[
            pltpu.VMEM(panel_shape, jnp.int32),
            pltpu.VMEM(col_shape, jnp.int32),
            pltpu.VMEM(row_shape, jnp.int32),
            pltpu.VMEM(panel_shape, jnp.int32),
            pltpu.VMEM(col_shape, jnp.int32),
            pltpu.SMEM(panel_shape, jnp.int32),
            pltpu.SMEM(col_shape, jnp.int32),
            pltpu.VMEM(teacher.shape, teacher.dtype),
            pltpu.VMEM((total * halves, LANES), jnp.float32),
            dma((n_col,)), dma((n_col,)), dma((n_row,)),
            dma((n_col,)), dma((groups,)), dma((n_row,)),
            dma((8,)), dma((8,)), dma((2,)), dma((2,)),
        ],
        compiler_params=pltpu.CompilerParams(
            collective_id=0, has_side_effects=True, vmem_limit_bytes=own_limit(teacher, inverse, total)
        ),
        name="exchange",
    )(*(pltpu.with_memory_space_constraint(x, pltpu.HBM) for x in operands))


def nt_dot(left, right):
    return lax.dot_general(left, right, (((1,), (1,)), ((), ())), preferred_element_type=jnp.float32)


def nn_dot(left, right):
    return lax.dot_general(left, right, (((1,), (0,)), ((), ())), preferred_element_type=jnp.float32)


def gram_kernel(
    n_row, n_col, stretch, emb_ref, rows_in, table_ref, inv_ref, norm_ref, trail_hbm, own_hbm,
    row_ids, picked, left_ref, cross_ref, fac_ref, back_ref, trail_ref,
    ids_sem, own_sem, trail_sem,
):
    width = inv_ref.shape[0]
    block = 256
    blocks = width // block
    embed = emb_ref.shape[1]
    halves = embed // LANES
    n_rows = n_col * stretch
    n_cols = n_row * stretch
    groups = n_col // n_row
    unit = unit_of(embed)
    row_at = lax.axis_index("row")
    col_at = lax.axis_index("col")
    tile = 512
    chunk = 64
    ring = picked.shape[0] // (chunk * halves)

    ids_move = pltpu.make_async_copy(rows_in, row_ids, ids_sem)
    ids_move.start()

    def inner(left, start, count):
        return nt_dot(left, emb_ref[start : start + count, :])

    def gaussian(product, left_norm, start, count):
        return jnp.exp2(product * (2.0 * unit) - (left_norm + norm_ref[0:1, start : start + count]))

    def pick(start, count):
        for base in range(start, start + count, chunk):
            home = base // chunk % ring * chunk
            for lane in range(chunk):
                q, place = divmod(base + lane, stretch)
                row = table_ref[pl.ds(row_ids[q % groups, q // groups, 0, place], halves), :]
                picked[(home + lane) * halves : (home + lane + 1) * halves, :] = row
            narrow(picked, left_ref, home, chunk, base)

    picked_rows, quiet = 0, blocks // 2
    hold = slice(tile, 2 * tile)
    for start in range(0, n_cols, tile):
        left = emb_ref[width + start : width + start + tile, :]
        left_norm = row_norm(left)
        rows = slice(start, start + tile)
        product = inner(left, 0, block)
        for at in range(blocks + 1):
            cols = slice((at - 1) * block, at * block)
            held = product
            if at < blocks:
                here = slice(at * block, (at + 1) * block)
                cross_ref[hold, here] = gaussian(held, left_norm, at * block, block).astype(jnp.bfloat16)
                if at + 1 < blocks:
                    product = inner(left, (at + 1) * block, block)
            if at:
                fac_ref[rows, cols] = nt_dot(
                    cross_ref[hold, : at * block], inv_ref[cols, : at * block]
                ).astype(jnp.bfloat16)
                if not start and at == quiet:
                    ids_move.wait()
                if not start and at >= quiet:
                    until = n_rows * (at - quiet + 1) // (blocks - quiet + 1) // chunk * chunk
                    pick(picked_rows, until - picked_rows)
                    picked_rows = until
    own = pltpu.make_async_copy(
        fac_ref.at[pl.ds(pl.multiple_of(row_at * stretch, stretch), stretch), :], own_hbm, own_sem
    )
    own.start()
    lefts = [(start, row_norm(left_ref[start : start + tile, :])) for start in range(0, n_rows, tile)]

    def cross_rows(tile_at, at):
        start, left_norm = lefts[tile_at]
        product = inner(left_ref[start : start + tile, :], at * block, block)
        value = gaussian(product, left_norm, at * block, block)
        home = tile_at % 2 * tile
        cross_ref[home : home + tile, at * block : (at + 1) * block] = value.astype(jnp.bfloat16)

    for at in range(blocks):
        cols = slice(at * block, (at + 1) * block)
        for tile_at in range(min(2, len(lefts))):
            cross_rows(tile_at, at)
        for start in range(0, n_cols, tile):
            rows = slice(start, start + tile)
            back_ref[rows, cols] = nn_dot(fac_ref[rows, at * block :], inv_ref[at * block :, cols]).astype(jnp.bfloat16)

    ahead = lax.broadcasted_iota(jnp.int32, (stretch, stretch), 0) - lax.broadcasted_iota(
        jnp.int32, (stretch, stretch), 1
    )
    pair = 2 if n_row % 2 == 0 else 1
    held_rows = tile * n_row

    def flush(at):
        return pltpu.make_async_copy(
            trail_ref.at[pl.ds(at % 2 * held_rows, held_rows)], trail_hbm.at[pl.ds(at * held_rows, held_rows)],
            trail_sem.at[at % 2],
        )

    for tile_at, (start, left_norm) in enumerate(lefts):
        left = left_ref[start : start + tile, :]
        last = (start + tile) // stretch - 1
        if tile_at >= 2:
            flush(tile_at - 2).wait()
            for at in range(blocks):
                cross_rows(tile_at, at)
        home = tile_at % 2 * tile
        for low in range(0, n_row, pair):
            if last * n_row + n_row - 1 >= low * n_col:
                span = slice(low * stretch, (low + pair) * stretch)
                first = width + low * stretch
                value = gaussian(inner(left, first, pair * stretch), left_norm, first, pair * stretch) - nt_dot(
                    cross_ref[home : home + tile, :], back_ref[span, :]
                )
            else:
                value = None
            for q in range(start // stretch, last + 1):
                for p in range(low, low + pair):
                    top = q * stretch - start
                    place = pl.ds(tile_at % 2 * held_rows + top * n_row + p, stretch, stride=n_row)
                    if q * n_row + n_row - 1 < p * n_col:
                        trail_ref[place, :] = jnp.zeros((stretch, stretch), jnp.float32)
                        continue
                    side = (p - low) * stretch
                    part = value[top : top + stretch, side : side + stretch]
                    if q * n_row < p * n_col + n_col:
                        gap = (p * n_col + col_at - q * n_row - row_at) * stretch
                        part = jnp.where(ahead >= gap, part, 0.0)
                    trail_ref[place, :] = part
        flush(tile_at).start()
    own.wait()
    for tile_at in range(max(len(lefts) - 2, 0), len(lefts)):
        flush(tile_at).wait()


def shards(teacher, panel_ids, rest_ids, inverse):
    n_row = lax.axis_size("row")
    n_col = lax.axis_size("col")
    stretch = rest_ids.shape[2]
    width = inverse.shape[0]
    emb, table, rows, inv, norms = exchange(rest_ids, panel_ids, teacher, inverse, n_row, n_col)
    n_rows = n_col * stretch
    n_cols = n_row * stretch
    embed = teacher.shape[1]
    halves = embed // LANES
    vmem = pl.BlockSpec(memory_space=pltpu.VMEM)
    hbm = pl.BlockSpec(memory_space=pltpu.HBM)
    dma = pltpu.SemaphoreType.DMA
    limit = own_limit(teacher, inverse, width + n_cols)
    held = 2 * n_rows * embed + 2048 * width + 4 * n_cols * width + 4096 * n_row * stretch + 9 * 1024 * 1024
    trailing, own_factor = pl.pallas_call(
        functools.partial(gram_kernel, n_row, n_col, stretch),
        out_shape=(
            jax.ShapeDtypeStruct((n_rows * n_row, stretch), jnp.float32),
            jax.ShapeDtypeStruct((stretch, width), jnp.bfloat16),
        ),
        in_specs=[vmem] * 5,
        out_specs=(hbm, hbm),
        scratch_shapes=[
            pltpu.SMEM(rows.shape, jnp.int32),
            pltpu.VMEM((512 * halves, LANES), jnp.float32),
            pltpu.VMEM((n_rows, embed), jnp.bfloat16),
            pltpu.VMEM((2 * 512, width), jnp.bfloat16),
            pltpu.VMEM((n_cols, width), jnp.bfloat16),
            pltpu.VMEM((n_cols, width), jnp.bfloat16),
            pltpu.VMEM((2 * 512 * n_row, stretch), jnp.float32),
            dma(()), dma(()), dma((2,)),
        ],
        compiler_params=pltpu.CompilerParams(vmem_limit_bytes=max(limit, held)),
        name="gram",
    )(emb, rows, table, inv, norms)
    return (
        trailing.reshape(n_col, 1, stretch, n_row, 1, stretch),
        own_factor.reshape(1, 1, stretch, width),
    )


def solution(mesh):
    return jax.shard_map(
        shards,
        mesh=mesh,
        in_specs=(P(), P("col"), P("row", "col", None), P()),
        out_specs=(P(None, "row", None, None, "col", None), P("row", "col", None, None)),
        check_vma=False,
    )
```

```python
import functools

import jax
import jax.numpy as jnp
from jax import lax
from jax.experimental import pallas as pl
from jax.experimental.pallas import tpu as pltpu
from jax.sharding import PartitionSpec as P

MESH = pl.DeviceIdType.MESH
LANES = 128
VMEM_BYTES = 67043328


def narrow(picked, out, first, count, at):
    halves = out.shape[1] // LANES
    for step in range(0, count, 64):
        for half in range(halves):
            value = picked[pl.ds((first + step) * halves + half, 64, stride=halves), :]
            out[at + step : at + step + 64, half * LANES : (half + 1) * LANES] = value.astype(jnp.bfloat16)


def unit_of(embed):
    return 2.0 / embed * 1.4426950408889634


def row_norm(value):
    return jnp.sum(jnp.square(value.astype(jnp.float32)), axis=-1, keepdims=True) * unit_of(value.shape[1])


def gaussian(product, left_norm, right_norm, embed):
    return jnp.exp2(product * (2.0 * unit_of(embed)) - (left_norm + right_norm))


def exchange_kernel(
    n_row, n_col, early, rest_hbm, panel_hbm, table_hbm, inv_hbm, emb_ref, table_ref, rows_out, inv_ref, norm_ref, cols_ref,
    panel_land, col_land, row_land, panel_scaled, col_scaled, panel_ids, col_ids, landed, picked,
    panel_send, row_send, col_send, panel_sem, row_sem, col_sem, table_sem, inv_sem, own_sem, ids_sem,
):
    pieces = table_sem.shape[0]
    halves = table_hbm.shape[1] // LANES
    piece = table_hbm.shape[0] // pieces
    width = panel_land.shape[2]
    stretch = col_land.shape[2]
    row_at = lax.axis_index("row")
    col_at = lax.axis_index("col")
    group = col_at // n_row
    forwards = lax.rem(col_at, n_row) == row_at

    own_panel = pltpu.make_async_copy(panel_hbm.at[0], panel_land.at[col_at], own_sem.at[0])
    own_col = pltpu.make_async_copy(rest_hbm.at[0], col_land.at[row_at], own_sem.at[1])
    own_panel.start()
    own_col.start()

    def load(at):
        rows = pl.ds(at * piece, piece)
        return pltpu.make_async_copy(table_hbm.at[rows], landed.at[rows], table_sem.at[at])

    def load_inverse(at):
        block = inv_hbm.shape[0] // pieces
        rows, cols = pl.ds(at * block, block), pl.ds(0, (at + 1) * block)
        return pltpu.make_async_copy(inv_hbm.at[rows, cols], inv_ref.at[rows, cols], inv_sem.at[at])

    for at in range(pieces):
        load(at).start()
    barrier = pltpu.get_barrier_semaphore()
    for step in range(1, n_row):
        other = lax.rem(row_at + step, n_row)
        pl.semaphore_signal(barrier, inc=1, device_id=(other, col_at), device_id_type=MESH)
    for step in range(1, n_col):
        other = lax.rem(col_at + step, n_col)
        pl.semaphore_signal(barrier, inc=1, device_id=(row_at, other), device_id_type=MESH)

    def widen(at):
        def body(step, carry):
            rows = pl.ds(pl.multiple_of(at * piece + step * 64, 64), 64)
            wide = landed[rows, :].astype(jnp.float32)
            for half in range(halves):
                place = pl.ds((at * piece + step * 64) * halves + half, 64, stride=halves)
                table_ref[place, :] = wide[:, half * LANES : (half + 1) * LANES]
            return carry

        load(at).wait()
        lax.fori_loop(0, piece // 64, body, 0)

    def panel_copy(slot, target):
        return pltpu.make_async_remote_copy(
            src_ref=panel_land.at[slot], dst_ref=panel_land.at[slot],
            send_sem=panel_send.at[target], recv_sem=panel_sem.at[slot],
            device_id=(row_at, target), device_id_type=MESH,
        )

    def row_copy(slot, target):
        return pltpu.make_async_remote_copy(
            src_ref=col_land, dst_ref=row_land.at[slot],
            send_sem=row_send.at[target], recv_sem=row_sem.at[slot],
            device_id=(row_at, target), device_id_type=MESH,
        )

    def col_copy(slot, target):
        return pltpu.make_async_remote_copy(
            src_ref=col_land.at[slot], dst_ref=col_land.at[slot],
            send_sem=col_send.at[target], recv_sem=col_sem.at[slot],
            device_id=(target, col_at), device_id_type=MESH,
        )

    def each(length, skip, act):
        for at in range(length):
            pl.when(jnp.logical_not(skip(at)))(functools.partial(act, at))

    own_panel.wait()
    own_col.wait()
    pl.semaphore_wait(barrier, n_row + n_col - 2)
    each(n_row, lambda at: at == row_at, lambda at: col_copy(row_at, at).start())
    each(n_col, lambda at: at == col_at, lambda at: panel_copy(col_at, at).start())
    for at in range(pieces // 2):
        widen(at)
    each(n_row, lambda at: at == row_at, lambda at: col_copy(at, at).wait_recv())
    keep = pltpu.make_async_copy(col_land, row_land.at[group], own_sem.at[0])

    @pl.when(forwards)
    def _():
        each(n_col, lambda at: at == col_at, lambda at: row_copy(group, at).start())
        keep.start()

    col_scaled[...] = col_land[...] * halves
    col_move = pltpu.make_async_copy(col_scaled, col_ids, ids_sem.at[0])
    col_move.start()
    for at in range(pieces):
        load_inverse(at).start()
    for at in range(pieces // 2, pieces):
        widen(at)
    each(n_col, lambda at: at == col_at, lambda at: panel_copy(at, at).wait_recv())
    panel_scaled[...] = panel_land[...] * halves
    panel_move = pltpu.make_async_copy(panel_scaled, panel_ids, ids_sem.at[1])
    panel_move.start()

    def pick(ids, block, span, start):
        for lane in range(span):
            place = (start + lane) * halves
            picked[place : place + halves, :] = table_ref[pl.ds(ids[block, 0, lane], halves), :]

    col_move.wait()
    first_col = n_col * width
    for block in range(n_row):
        pick(col_ids, block, stretch, first_col + block * stretch)
    narrow(picked, emb_ref, first_col, n_row * stretch, first_col)
    panel_move.wait()
    for block in range(n_col):
        pick(panel_ids, block, width, block * width)
        if block:
            narrow(picked, emb_ref, (block - 1) * width, width, (block - 1) * width)
    narrow(picked, emb_ref, (n_col - 1) * width, width, (n_col - 1) * width)
    eye = lax.broadcasted_iota(jnp.int32, (LANES, LANES), 0) == lax.broadcasted_iota(jnp.int32, (LANES, LANES), 1)
    for at in range(0, emb_ref.shape[0], LANES):
        norm = jnp.broadcast_to(row_norm(emb_ref[at : at + LANES, :]), (LANES, LANES))
        norm_ref[0:1, at : at + LANES] = jnp.sum(jnp.where(eye, norm, 0.0), axis=0, keepdims=True)

    if early:
        embed = emb_ref.shape[1]
        left = emb_ref[first_col : first_col + n_row * stretch, :]
        left_norm = row_norm(left)
        for at in range(0, first_col, 256):
            cols = slice(at, at + 256)
            value = gaussian(nt_dot(left, emb_ref[cols, :]), left_norm, norm_ref[0:1, cols], embed)
            cols_ref[:, cols] = value.astype(jnp.bfloat16)

    @pl.when(forwards)
    def _():
        keep.wait()

    for slot in range(n_col // n_row):
        source = slot * n_row + row_at

        @pl.when(source != col_at)
        def _(slot=slot, source=source):
            row_copy(slot, source).wait_recv()

    rows_out[...] = row_land[...] * halves
    for at in range(pieces):
        load_inverse(at).wait()
    each(n_row, lambda at: at == row_at, lambda at: col_copy(row_at, at).wait_send())
    each(n_col, lambda at: at == col_at, lambda at: panel_copy(col_at, at).wait_send())

    @pl.when(forwards)
    def _():
        each(n_col, lambda at: at == col_at, lambda at: row_copy(group, at).wait_send())


def is_early(n_cols):
    return n_cols == 512


def own_limit(teacher, inverse, total):
    n_cols = total - inverse.shape[0]
    early = 2 * n_cols * inverse.shape[0] if is_early(n_cols) else 0
    return VMEM_BYTES - 4 * teacher.size - 2 * inverse.size - 2 * total * teacher.shape[1] - early - 12 * 1024 * 1024


def exchange(rest_ids, panel_ids, teacher, inverse, n_row, n_col):
    stretch = rest_ids.shape[2]
    width = panel_ids.shape[0]
    total = n_col * width + n_row * stretch
    halves = teacher.shape[1] // LANES
    groups = n_col // n_row
    panel_shape = (n_col, 1, width)
    col_shape = (n_row, 1, stretch)
    row_shape = (groups, n_row, 1, stretch)
    vmem = pl.BlockSpec(memory_space=pltpu.VMEM)
    hbm = pl.BlockSpec(memory_space=pltpu.HBM)
    dma = pltpu.SemaphoreType.DMA
    early = is_early(n_row * stretch)
    operands = (rest_ids, panel_ids.reshape(1, 1, width), teacher, inverse)
    return pl.pallas_call(
        functools.partial(exchange_kernel, n_row, n_col, early),
        out_shape=(
            jax.ShapeDtypeStruct((total, teacher.shape[1]), teacher.dtype),
            jax.ShapeDtypeStruct((teacher.shape[0] * halves, LANES), jnp.float32),
            jax.ShapeDtypeStruct(row_shape, jnp.int32),
            jax.ShapeDtypeStruct(inverse.shape, inverse.dtype),
            jax.ShapeDtypeStruct((8, total), jnp.float32),
            jax.ShapeDtypeStruct((n_row * stretch if early else 16, inverse.shape[0]), teacher.dtype),
        ),
        in_specs=[hbm] * 4,
        out_specs=(vmem,) * 6,
        scratch_shapes=[
            pltpu.VMEM(panel_shape, jnp.int32),
            pltpu.VMEM(col_shape, jnp.int32),
            pltpu.VMEM(row_shape, jnp.int32),
            pltpu.VMEM(panel_shape, jnp.int32),
            pltpu.VMEM(col_shape, jnp.int32),
            pltpu.SMEM(panel_shape, jnp.int32),
            pltpu.SMEM(col_shape, jnp.int32),
            pltpu.VMEM(teacher.shape, teacher.dtype),
            pltpu.VMEM((total * halves, LANES), jnp.float32),
            dma((n_col,)), dma((n_col,)), dma((n_row,)),
            dma((n_col,)), dma((groups,)), dma((n_row,)),
            dma((8,)), dma((8,)), dma((2,)), dma((2,)),
        ],
        compiler_params=pltpu.CompilerParams(
            collective_id=0, has_side_effects=True, vmem_limit_bytes=own_limit(teacher, inverse, total)
        ),
        name="exchange",
    )(*(pltpu.with_memory_space_constraint(x, pltpu.HBM) for x in operands))


def nt_dot(left, right):
    return lax.dot_general(left, right, (((1,), (1,)), ((), ())), preferred_element_type=jnp.float32)


def nn_dot(left, right):
    return lax.dot_general(left, right, (((1,), (0,)), ((), ())), preferred_element_type=jnp.float32)


def gram_kernel(
    n_row, n_col, stretch, emb_ref, rows_in, table_ref, inv_ref, norm_ref, cols_ref, trail_hbm, own_hbm,
    row_ids, picked, left_ref, cross_ref, fac_ref, back_ref, trail_ref,
    ids_sem, own_sem, trail_sem,
):
    width = inv_ref.shape[0]
    block = 256
    blocks = width // block
    embed = emb_ref.shape[1]
    halves = embed // LANES
    n_rows = n_col * stretch
    n_cols = n_row * stretch
    groups = n_col // n_row
    row_at = lax.axis_index("row")
    col_at = lax.axis_index("col")
    tile = 512
    chunk = 64
    ring = picked.shape[0] // (chunk * halves)

    ids_move = pltpu.make_async_copy(rows_in, row_ids, ids_sem)
    ids_move.start()

    def inner(left, start, count):
        return nt_dot(left, emb_ref[start : start + count, :])

    def gauss(left, left_norm, start, count):
        return gaussian(inner(left, start, count), left_norm, norm_ref[0:1, start : start + count], embed)

    def pick(start, count):
        for base in range(start, start + count, chunk):
            home = base // chunk % ring * chunk
            for lane in range(chunk):
                q, place = divmod(base + lane, stretch)
                row = table_ref[pl.ds(row_ids[q % groups, q // groups, 0, place], halves), :]
                picked[(home + lane) * halves : (home + lane + 1) * halves, :] = row
            narrow(picked, left_ref, home, chunk, base)

    picked_rows, quiet = 0, blocks // 2
    early = is_early(n_cols)
    hold = slice(0, tile) if early else slice(tile, 2 * tile)
    crosses = cols_ref if early else cross_ref
    for start in range(0, n_cols, tile):
        rows = slice(start, start + tile)
        if not early:
            left = emb_ref[width + start : width + start + tile, :]
            left_norm = row_norm(left)
        for at in range(blocks + 1):
            cols = slice((at - 1) * block, at * block)
            if at < blocks and not early:
                value = gauss(left, left_norm, at * block, block)
                cross_ref[hold, at * block : (at + 1) * block] = value.astype(jnp.bfloat16)
            if at:
                fac_ref[rows, cols] = nt_dot(
                    crosses[hold, : at * block], inv_ref[cols, : at * block]
                ).astype(jnp.bfloat16)
                if not start and at == quiet:
                    ids_move.wait()
                if not start and at >= quiet:
                    until = n_rows * (at - quiet + 1) // (blocks - quiet + 1) // chunk * chunk
                    pick(picked_rows, until - picked_rows)
                    picked_rows = until
    own = pltpu.make_async_copy(
        fac_ref.at[pl.ds(pl.multiple_of(row_at * stretch, stretch), stretch), :], own_hbm, own_sem
    )
    own.start()
    lefts = [(start, row_norm(left_ref[start : start + tile, :])) for start in range(0, n_rows, tile)]

    def cross_rows(tile_at, at):
        start, left_norm = lefts[tile_at]
        value = gauss(left_ref[start : start + tile, :], left_norm, at * block, block)
        home = tile_at % 2 * tile
        cross_ref[home : home + tile, at * block : (at + 1) * block] = value.astype(jnp.bfloat16)

    for at in range(blocks):
        cols = slice(at * block, (at + 1) * block)
        for tile_at in range(min(2, len(lefts))):
            cross_rows(tile_at, at)
        for start in range(0, n_cols, tile):
            rows = slice(start, start + tile)
            back_ref[rows, cols] = nn_dot(fac_ref[rows, at * block :], inv_ref[at * block :, cols]).astype(jnp.bfloat16)

    ahead = lax.broadcasted_iota(jnp.int32, (stretch, stretch), 0) - lax.broadcasted_iota(
        jnp.int32, (stretch, stretch), 1
    )
    pair = 2 if n_row % 2 == 0 else 1
    held_rows = tile * n_row

    def flush(at):
        return pltpu.make_async_copy(
            trail_ref.at[pl.ds(at % 2 * held_rows, held_rows)], trail_hbm.at[pl.ds(at * held_rows, held_rows)],
            trail_sem.at[at % 2],
        )

    for tile_at, (start, left_norm) in enumerate(lefts):
        left = left_ref[start : start + tile, :]
        last = (start + tile) // stretch - 1
        if tile_at >= 2:
            flush(tile_at - 2).wait()
            for at in range(blocks):
                cross_rows(tile_at, at)
        home = tile_at % 2 * tile
        for low in range(0, n_row, pair):
            if last * n_row + n_row - 1 >= low * n_col:
                span = slice(low * stretch, (low + pair) * stretch)
                first = width + low * stretch
                value = gauss(left, left_norm, first, pair * stretch) - nt_dot(
                    cross_ref[home : home + tile, :], back_ref[span, :]
                )
            else:
                value = None
            for q in range(start // stretch, last + 1):
                for p in range(low, low + pair):
                    top = q * stretch - start
                    place = pl.ds(tile_at % 2 * held_rows + top * n_row + p, stretch, stride=n_row)
                    if q * n_row + n_row - 1 < p * n_col:
                        trail_ref[place, :] = jnp.zeros((stretch, stretch), jnp.float32)
                        continue
                    side = (p - low) * stretch
                    part = value[top : top + stretch, side : side + stretch]
                    if q * n_row < p * n_col + n_col:
                        gap = (p * n_col + col_at - q * n_row - row_at) * stretch
                        part = jnp.where(ahead >= gap, part, 0.0)
                    trail_ref[place, :] = part
        flush(tile_at).start()
    own.wait()
    for tile_at in range(max(len(lefts) - 2, 0), len(lefts)):
        flush(tile_at).wait()


def shards(teacher, panel_ids, rest_ids, inverse):
    n_row = lax.axis_size("row")
    n_col = lax.axis_size("col")
    stretch = rest_ids.shape[2]
    width = inverse.shape[0]
    emb, table, rows, inv, norms, crosses = exchange(rest_ids, panel_ids, teacher, inverse, n_row, n_col)
    n_rows = n_col * stretch
    n_cols = n_row * stretch
    embed = teacher.shape[1]
    halves = embed // LANES
    vmem = pl.BlockSpec(memory_space=pltpu.VMEM)
    hbm = pl.BlockSpec(memory_space=pltpu.HBM)
    dma = pltpu.SemaphoreType.DMA
    limit = own_limit(teacher, inverse, width + n_cols)
    held = 2 * n_rows * embed + 2048 * width + 4 * n_cols * width + 4096 * n_row * stretch + 9 * 1024 * 1024
    trailing, own_factor = pl.pallas_call(
        functools.partial(gram_kernel, n_row, n_col, stretch),
        out_shape=(
            jax.ShapeDtypeStruct((n_rows * n_row, stretch), jnp.float32),
            jax.ShapeDtypeStruct((stretch, width), jnp.bfloat16),
        ),
        in_specs=[vmem] * 6,
        out_specs=(hbm, hbm),
        scratch_shapes=[
            pltpu.SMEM(rows.shape, jnp.int32),
            pltpu.VMEM((512 * halves, LANES), jnp.float32),
            pltpu.VMEM((n_rows, embed), jnp.bfloat16),
            pltpu.VMEM((2 * 512, width), jnp.bfloat16),
            pltpu.VMEM((n_cols, width), jnp.bfloat16),
            pltpu.VMEM((n_cols, width), jnp.bfloat16),
            pltpu.VMEM((2 * 512 * n_row, stretch), jnp.float32),
            dma(()), dma(()), dma((2,)),
        ],
        compiler_params=pltpu.CompilerParams(vmem_limit_bytes=max(limit, held)),
        name="gram",
    )(emb, rows, table, inv, norms, crosses)
    return (
        trailing.reshape(n_col, 1, stretch, n_row, 1, stretch),
        own_factor.reshape(1, 1, stretch, width),
    )


def solution(mesh):
    return jax.shard_map(
        shards,
        mesh=mesh,
        in_specs=(P(), P("col"), P("row", "col", None), P()),
        out_specs=(P(None, "row", None, None, "col", None), P("row", "col", None, None)),
        check_vma=False,
    )
```

```python
import functools

import jax
import jax.numpy as jnp
from jax import lax
from jax.experimental import pallas as pl
from jax.experimental.pallas import tpu as pltpu
from jax.sharding import PartitionSpec as P

MESH = pl.DeviceIdType.MESH
LANES = 128
VMEM_BYTES = 67043328


def narrow(picked, out, first, count, at):
    halves = out.shape[1] // LANES
    for step in range(0, count, 64):
        for half in range(halves):
            value = picked[pl.ds((first + step) * halves + half, 64, stride=halves), :]
            out[at + step : at + step + 64, half * LANES : (half + 1) * LANES] = value.astype(jnp.bfloat16)


def unit_of(embed):
    return 2.0 / embed * 1.4426950408889634


def row_norm(value):
    return jnp.sum(jnp.square(value.astype(jnp.float32)), axis=-1, keepdims=True) * unit_of(value.shape[1])


def gaussian(product, left_norm, right_norm, embed):
    return jnp.exp2(product * (2.0 * unit_of(embed)) - (left_norm + right_norm))


def exchange_kernel(
    n_row, n_col, early, rest_hbm, panel_hbm, table_hbm, inv_hbm, emb_ref, table_ref, rows_out, inv_ref, norm_ref, cols_ref,
    panel_land, col_land, row_land, panel_scaled, col_scaled, panel_ids, col_ids, landed, picked,
    panel_send, row_send, col_send, panel_sem, row_sem, col_sem, table_sem, inv_sem, own_sem, ids_sem,
):
    pieces = table_sem.shape[0]
    halves = table_hbm.shape[1] // LANES
    piece = table_hbm.shape[0] // pieces
    width = panel_land.shape[2]
    stretch = col_land.shape[2]
    row_at = lax.axis_index("row")
    col_at = lax.axis_index("col")
    group = col_at // n_row
    forwards = lax.rem(col_at, n_row) == row_at

    own_panel = pltpu.make_async_copy(panel_hbm.at[0], panel_land.at[col_at], own_sem.at[0])
    own_col = pltpu.make_async_copy(rest_hbm.at[0], col_land.at[row_at], own_sem.at[1])
    own_panel.start()
    own_col.start()

    def load(at):
        rows = pl.ds(at * piece, piece)
        return pltpu.make_async_copy(table_hbm.at[rows], landed.at[rows], table_sem.at[at])

    def load_inverse(at):
        block = inv_hbm.shape[0] // pieces
        rows, cols = pl.ds(at * block, block), pl.ds(0, (at + 1) * block)
        return pltpu.make_async_copy(inv_hbm.at[rows, cols], inv_ref.at[rows, cols], inv_sem.at[at])

    for at in range(pieces):
        load(at).start()
    barrier = pltpu.get_barrier_semaphore()
    for step in range(1, n_row):
        other = lax.rem(row_at + step, n_row)
        pl.semaphore_signal(barrier, inc=1, device_id=(other, col_at), device_id_type=MESH)
    for step in range(1, n_col):
        other = lax.rem(col_at + step, n_col)
        pl.semaphore_signal(barrier, inc=1, device_id=(row_at, other), device_id_type=MESH)

    def widen(at):
        def body(step, carry):
            rows = pl.ds(pl.multiple_of(at * piece + step * 64, 64), 64)
            wide = landed[rows, :].astype(jnp.float32)
            for half in range(halves):
                place = pl.ds((at * piece + step * 64) * halves + half, 64, stride=halves)
                table_ref[place, :] = wide[:, half * LANES : (half + 1) * LANES]
            return carry

        load(at).wait()
        lax.fori_loop(0, piece // 64, body, 0)

    def panel_copy(slot, target):
        return pltpu.make_async_remote_copy(
            src_ref=panel_land.at[slot], dst_ref=panel_land.at[slot],
            send_sem=panel_send.at[target], recv_sem=panel_sem.at[slot],
            device_id=(row_at, target), device_id_type=MESH,
        )

    def row_copy(slot, target):
        return pltpu.make_async_remote_copy(
            src_ref=col_land, dst_ref=row_land.at[slot],
            send_sem=row_send.at[target], recv_sem=row_sem.at[slot],
            device_id=(row_at, target), device_id_type=MESH,
        )

    def col_copy(slot, target):
        return pltpu.make_async_remote_copy(
            src_ref=col_land.at[slot], dst_ref=col_land.at[slot],
            send_sem=col_send.at[target], recv_sem=col_sem.at[slot],
            device_id=(target, col_at), device_id_type=MESH,
        )

    def each(length, skip, act):
        for at in range(length):
            pl.when(jnp.logical_not(skip(at)))(functools.partial(act, at))

    own_panel.wait()
    own_col.wait()
    pl.semaphore_wait(barrier, n_row + n_col - 2)
    each(n_row, lambda at: at == row_at, lambda at: col_copy(row_at, at).start())
    each(n_col, lambda at: at == col_at, lambda at: panel_copy(col_at, at).start())
    for at in range(pieces // 2):
        widen(at)
    each(n_row, lambda at: at == row_at, lambda at: col_copy(at, at).wait_recv())
    keep = pltpu.make_async_copy(col_land, row_land.at[group], own_sem.at[0])

    @pl.when(forwards)
    def _():
        each(n_col, lambda at: at == col_at, lambda at: row_copy(group, at).start())
        keep.start()

    col_scaled[...] = col_land[...] * halves
    col_move = pltpu.make_async_copy(col_scaled, col_ids, ids_sem.at[0])
    col_move.start()
    for at in range(pieces):
        load_inverse(at).start()
    for at in range(pieces // 2, pieces):
        widen(at)
    each(n_col, lambda at: at == col_at, lambda at: panel_copy(at, at).wait_recv())
    panel_scaled[...] = panel_land[...] * halves
    panel_move = pltpu.make_async_copy(panel_scaled, panel_ids, ids_sem.at[1])
    panel_move.start()

    def pick(ids, block, span, start):
        for lane in range(span):
            place = (start + lane) * halves
            picked[place : place + halves, :] = table_ref[pl.ds(ids[block, 0, lane], halves), :]

    col_move.wait()
    first_col = n_col * width
    for block in range(n_row):
        pick(col_ids, block, stretch, first_col + block * stretch)
    narrow(picked, emb_ref, first_col, n_row * stretch, first_col)
    panel_move.wait()
    for block in range(n_col):
        pick(panel_ids, block, width, block * width)
        if block:
            narrow(picked, emb_ref, (block - 1) * width, width, (block - 1) * width)
    narrow(picked, emb_ref, (n_col - 1) * width, width, (n_col - 1) * width)
    eye = lax.broadcasted_iota(jnp.int32, (LANES, LANES), 0) == lax.broadcasted_iota(jnp.int32, (LANES, LANES), 1)
    for at in range(0, emb_ref.shape[0], LANES):
        norm = jnp.broadcast_to(row_norm(emb_ref[at : at + LANES, :]), (LANES, LANES))
        norm_ref[0:1, at : at + LANES] = jnp.sum(jnp.where(eye, norm, 0.0), axis=0, keepdims=True)

    if early:
        embed = emb_ref.shape[1]
        left = emb_ref[first_col : first_col + n_row * stretch, :]
        left_norm = row_norm(left)
        for at in range(0, first_col, 256):
            cols = slice(at, at + 256)
            value = gaussian(nt_dot(left, emb_ref[cols, :]), left_norm, norm_ref[0:1, cols], embed)
            cols_ref[:, cols] = value.astype(jnp.bfloat16)

    @pl.when(forwards)
    def _():
        keep.wait()

    for slot in range(n_col // n_row):
        source = slot * n_row + row_at

        @pl.when(source != col_at)
        def _(slot=slot, source=source):
            row_copy(slot, source).wait_recv()

    rows_out[...] = row_land[...] * halves
    for at in range(pieces):
        load_inverse(at).wait()
    each(n_row, lambda at: at == row_at, lambda at: col_copy(row_at, at).wait_send())
    each(n_col, lambda at: at == col_at, lambda at: panel_copy(col_at, at).wait_send())

    @pl.when(forwards)
    def _():
        each(n_col, lambda at: at == col_at, lambda at: row_copy(group, at).wait_send())


def is_early(n_cols):
    return n_cols == 512


def own_limit(teacher, inverse, total):
    n_cols = total - inverse.shape[0]
    early = 2 * n_cols * inverse.shape[0] if is_early(n_cols) else 0
    return VMEM_BYTES - 4 * teacher.size - 2 * inverse.size - 2 * total * teacher.shape[1] - early - 12 * 1024 * 1024


def exchange(rest_ids, panel_ids, teacher, inverse, n_row, n_col):
    stretch = rest_ids.shape[2]
    width = panel_ids.shape[0]
    total = n_col * width + n_row * stretch
    halves = teacher.shape[1] // LANES
    groups = n_col // n_row
    panel_shape = (n_col, 1, width)
    col_shape = (n_row, 1, stretch)
    row_shape = (groups, n_row, 1, stretch)
    vmem = pl.BlockSpec(memory_space=pltpu.VMEM)
    hbm = pl.BlockSpec(memory_space=pltpu.HBM)
    dma = pltpu.SemaphoreType.DMA
    early = is_early(n_row * stretch)
    operands = (rest_ids, panel_ids.reshape(1, 1, width), teacher, inverse)
    return pl.pallas_call(
        functools.partial(exchange_kernel, n_row, n_col, early),
        out_shape=(
            jax.ShapeDtypeStruct((total, teacher.shape[1]), teacher.dtype),
            jax.ShapeDtypeStruct((teacher.shape[0] * halves, LANES), jnp.float32),
            jax.ShapeDtypeStruct(row_shape, jnp.int32),
            jax.ShapeDtypeStruct(inverse.shape, inverse.dtype),
            jax.ShapeDtypeStruct((8, total), jnp.float32),
            jax.ShapeDtypeStruct((n_row * stretch if early else 16, inverse.shape[0]), teacher.dtype),
        ),
        in_specs=[hbm] * 4,
        out_specs=(vmem,) * 6,
        scratch_shapes=[
            pltpu.VMEM(panel_shape, jnp.int32),
            pltpu.VMEM(col_shape, jnp.int32),
            pltpu.VMEM(row_shape, jnp.int32),
            pltpu.VMEM(panel_shape, jnp.int32),
            pltpu.VMEM(col_shape, jnp.int32),
            pltpu.SMEM(panel_shape, jnp.int32),
            pltpu.SMEM(col_shape, jnp.int32),
            pltpu.VMEM(teacher.shape, teacher.dtype),
            pltpu.VMEM((total * halves, LANES), jnp.float32),
            dma((n_col,)), dma((n_col,)), dma((n_row,)),
            dma((n_col,)), dma((groups,)), dma((n_row,)),
            dma((8,)), dma((8,)), dma((2,)), dma((2,)),
        ],
        compiler_params=pltpu.CompilerParams(
            collective_id=0, has_side_effects=True, vmem_limit_bytes=own_limit(teacher, inverse, total)
        ),
        name="exchange",
    )(*(pltpu.with_memory_space_constraint(x, pltpu.HBM) for x in operands))


def nt_dot(left, right):
    return lax.dot_general(left, right, (((1,), (1,)), ((), ())), preferred_element_type=jnp.float32)


def nn_dot(left, right):
    return lax.dot_general(left, right, (((1,), (0,)), ((), ())), preferred_element_type=jnp.float32)


def gram_kernel(
    n_row, n_col, stretch, emb_ref, rows_in, table_ref, inv_ref, norm_ref, cols_ref, trail_hbm, own_hbm,
    row_ids, picked, left_ref, cross_ref, fac_ref, back_ref, trail_ref,
    ids_sem, own_sem, trail_sem,
):
    width = inv_ref.shape[0]
    block = 256
    blocks = width // block
    embed = emb_ref.shape[1]
    halves = embed // LANES
    n_rows = n_col * stretch
    n_cols = n_row * stretch
    groups = n_col // n_row
    row_at = lax.axis_index("row")
    col_at = lax.axis_index("col")
    tile = 512
    chunk = 64
    ring = picked.shape[0] // (chunk * halves)

    ids_move = pltpu.make_async_copy(rows_in, row_ids, ids_sem)
    ids_move.start()

    def inner(left, start, count):
        return nt_dot(left, emb_ref[start : start + count, :])

    def gauss(left, left_norm, start, count):
        return gaussian(inner(left, start, count), left_norm, norm_ref[0:1, start : start + count], embed)

    def pick(start, count):
        for base in range(start, start + count, chunk):
            home = base // chunk % ring * chunk
            for lane in range(chunk):
                q, place = divmod(base + lane, stretch)
                row = table_ref[pl.ds(row_ids[q % groups, q // groups, 0, place], halves), :]
                picked[(home + lane) * halves : (home + lane + 1) * halves, :] = row
            narrow(picked, left_ref, home, chunk, base)

    picked_rows, quiet = 0, blocks // 2
    early = is_early(n_cols)
    hold = slice(0, tile) if early else slice(tile, 2 * tile)
    crosses = cols_ref if early else cross_ref
    for start in range(0, n_cols, tile):
        if not early:
            left = emb_ref[width + start : width + start + tile, :]
            left_norm = row_norm(left)
        for at in range(blocks + 1):
            cols = slice((at - 1) * block, at * block)
            if at < blocks and not early:
                value = gauss(left, left_norm, at * block, block)
                cross_ref[hold, at * block : (at + 1) * block] = value.astype(jnp.bfloat16)
            if at:
                for part in (0, tile // 2):
                    fac_ref[start + part : start + part + tile // 2, cols] = nt_dot(
                        crosses[hold.start + part : hold.start + part + tile // 2, : at * block],
                        inv_ref[cols, : at * block],
                    ).astype(jnp.bfloat16)
                if not start and at == quiet:
                    ids_move.wait()
                if not start and at >= quiet:
                    until = n_rows * (at - quiet + 1) // (blocks - quiet + 1) // chunk * chunk
                    pick(picked_rows, until - picked_rows)
                    picked_rows = until
    own = pltpu.make_async_copy(
        fac_ref.at[pl.ds(pl.multiple_of(row_at * stretch, stretch), stretch), :], own_hbm, own_sem
    )
    own.start()
    lefts = [(start, row_norm(left_ref[start : start + tile, :])) for start in range(0, n_rows, tile)]

    def cross_rows(tile_at, at):
        start, left_norm = lefts[tile_at]
        value = gauss(left_ref[start : start + tile, :], left_norm, at * block, block)
        home = tile_at % 2 * tile
        cross_ref[home : home + tile, at * block : (at + 1) * block] = value.astype(jnp.bfloat16)

    for at in range(blocks):
        cols = slice(at * block, (at + 1) * block)
        for tile_at in range(min(2, len(lefts))):
            cross_rows(tile_at, at)
        for start in range(0, n_cols, tile):
            rows = slice(start, start + tile)
            back_ref[rows, cols] = nn_dot(fac_ref[rows, at * block :], inv_ref[at * block :, cols]).astype(jnp.bfloat16)

    ahead = lax.broadcasted_iota(jnp.int32, (stretch, stretch), 0) - lax.broadcasted_iota(
        jnp.int32, (stretch, stretch), 1
    )
    pair = 2 if n_row % 2 == 0 else 1
    held_rows = tile * n_row

    def flush(at):
        return pltpu.make_async_copy(
            trail_ref.at[pl.ds(at % 2 * held_rows, held_rows)], trail_hbm.at[pl.ds(at * held_rows, held_rows)],
            trail_sem.at[at % 2],
        )

    for tile_at, (start, left_norm) in enumerate(lefts):
        left = left_ref[start : start + tile, :]
        last = (start + tile) // stretch - 1
        if tile_at >= 2:
            flush(tile_at - 2).wait()
            for at in range(blocks):
                cross_rows(tile_at, at)
        home = tile_at % 2 * tile
        for low in range(0, n_row, pair):
            if last * n_row + n_row - 1 >= low * n_col:
                span = slice(low * stretch, (low + pair) * stretch)
                first = width + low * stretch
                half = tile // 2
                value = [
                    gauss(left[part : part + half], left_norm[part : part + half], first, pair * stretch)
                    - nt_dot(cross_ref[home + part : home + part + half, :], back_ref[span, :])
                    for part in (0, half)
                ]
            else:
                value = None
            for q in range(start // stretch, last + 1):
                for p in range(low, low + pair):
                    top = q * stretch - start
                    place = pl.ds(tile_at % 2 * held_rows + top * n_row + p, stretch, stride=n_row)
                    if q * n_row + n_row - 1 < p * n_col:
                        trail_ref[place, :] = jnp.zeros((stretch, stretch), jnp.float32)
                        continue
                    side = (p - low) * stretch
                    part = value[top // half][top % half : top % half + stretch, side : side + stretch]
                    if q * n_row < p * n_col + n_col:
                        gap = (p * n_col + col_at - q * n_row - row_at) * stretch
                        part = jnp.where(ahead >= gap, part, 0.0)
                    trail_ref[place, :] = part
        flush(tile_at).start()
    own.wait()
    for tile_at in range(max(len(lefts) - 2, 0), len(lefts)):
        flush(tile_at).wait()


def shards(teacher, panel_ids, rest_ids, inverse):
    n_row = lax.axis_size("row")
    n_col = lax.axis_size("col")
    stretch = rest_ids.shape[2]
    width = inverse.shape[0]
    emb, table, rows, inv, norms, crosses = exchange(rest_ids, panel_ids, teacher, inverse, n_row, n_col)
    n_rows = n_col * stretch
    n_cols = n_row * stretch
    embed = teacher.shape[1]
    halves = embed // LANES
    vmem = pl.BlockSpec(memory_space=pltpu.VMEM)
    hbm = pl.BlockSpec(memory_space=pltpu.HBM)
    dma = pltpu.SemaphoreType.DMA
    limit = own_limit(teacher, inverse, width + n_cols)
    held = 2 * n_rows * embed + 2048 * width + 4 * n_cols * width + 4096 * n_row * stretch + 9 * 1024 * 1024
    trailing, own_factor = pl.pallas_call(
        functools.partial(gram_kernel, n_row, n_col, stretch),
        out_shape=(
            jax.ShapeDtypeStruct((n_rows * n_row, stretch), jnp.float32),
            jax.ShapeDtypeStruct((stretch, width), jnp.bfloat16),
        ),
        in_specs=[vmem] * 6,
        out_specs=(hbm, hbm),
        scratch_shapes=[
            pltpu.SMEM(rows.shape, jnp.int32),
            pltpu.VMEM((512 * halves, LANES), jnp.float32),
            pltpu.VMEM((n_rows, embed), jnp.bfloat16),
            pltpu.VMEM((2 * 512, width), jnp.bfloat16),
            pltpu.VMEM((n_cols, width), jnp.bfloat16),
            pltpu.VMEM((n_cols, width), jnp.bfloat16),
            pltpu.VMEM((2 * 512 * n_row, stretch), jnp.float32),
            dma(()), dma(()), dma((2,)),
        ],
        compiler_params=pltpu.CompilerParams(vmem_limit_bytes=max(limit, held)),
        name="gram",
    )(emb, rows, table, inv, norms, crosses)
    return (
        trailing.reshape(n_col, 1, stretch, n_row, 1, stretch),
        own_factor.reshape(1, 1, stretch, width),
    )


def solution(mesh):
    return jax.shard_map(
        shards,
        mesh=mesh,
        in_specs=(P(), P("col"), P("row", "col", None), P()),
        out_specs=(P(None, "row", None, None, "col", None), P("row", "col", None, None)),
        check_vma=False,
    )
```
